32 devices in a mesh: grp: 2 (over y), freq: 4 (over z), panel: 4 (over x, core).
Axes of the slice: x: 2, y: 2, z: 4, core: 2. Of those that a mesh axis runs over, the one named last changes fastest.
Arguments:
- traces: float32 [1024, 3072], P('freq', ('grp', 'panel')), parts along dimension 1, may hold values from -6 to 6
- centroids: float32 [3, 3072], P(None, ('grp', 'panel')), parts along dimension 1, may hold values from -1 to 1
- near_list: int32 [8, 8, 2], P(('grp', 'panel')), parts along dimension 0, may hold values from 0 to 4, as said below
- pair_count: int32 [8], P(('grp', 'panel')), parts along dimension 0, may hold values from 5 to 8, as said below
Outputs:
- field: float32 [1024, 3072], P('freq', ('grp', 'panel')), parts along dimension 1
The draws below stay inside these ranges and needn't reach their ends.
There are 2 independent parts, one for each index of `grp`. The reference program is written for one: setup_inputs(seed, part) draws one part's arguments, and reference() takes and returns one part's arrays. A program takes and returns all parts, laid end to end along the dimension named above; each array names one. Nothing has to cross between parts.
Inputs may be any that keep to these rules, and one draw needn't show every extreme that they name: `near_list`: each row holds a row block below 3 and an extended column block up to 4; in every shard, pair n < 3 is (n, n + 1), pair 3 is (0, 0) and pair 4 is (2, 4); pairs may repeat; entries past the count are valid but unused. `pair_count`: some shard holds 8 pairs in every draw.
All inputs are finite; a program needn't handle non-finite values.
Results may differ from the reference program's by a relative error of at most 0.0003.
Values sent between devices are 32-bit elements; how exact they have to be, the bound alone decides.
A program may use at most 64 MiB of HBM per device.

```python
import math
import jax
import jax.numpy as jnp
from jax import lax

NT = 1024
BLK = 128
NB = 3
MAXP = 8
PD = 384
SHARDS = 4
NP = 1536
KH = 512
N_PANEL = 4


def pair_tables(key):
    base = jax.random.fold_in(key, 11)
    key_extra, key_top, key_rows, key_cols = jax.random.split(base, 4)
    extra = jax.random.randint(key_extra, (SHARDS,), 2, MAXP - NB + 1)
    chosen = jax.random.randint(key_top, (), 0, SHARDS)
    extra = jnp.where(jnp.arange(SHARDS) == chosen, MAXP - NB, extra)
    counts = (NB + extra).astype(jnp.int32)
    rows = jax.random.randint(key_rows, (SHARDS, MAXP), 0, NB)
    cols = jax.random.randint(key_cols, (SHARDS, MAXP), 0, NB + 2)
    slot = jnp.arange(MAXP)[None, :] + jnp.zeros((SHARDS, 1), jnp.int32)
    rows = jnp.where(slot < NB, slot, rows)
    cols = jnp.where(slot < NB, slot + 1, cols)
    rows = jnp.where(slot == NB, 0, rows)
    cols = jnp.where(slot == NB, 0, cols)
    rows = jnp.where(slot == NB + 1, NB - 1, rows)
    cols = jnp.where(slot == NB + 1, NB + 1, cols)
    return (jnp.stack([rows, cols], axis=-1).astype(jnp.int32), counts)


def draw_near_list(key, part):
    return pair_tables(key)[0]


def draw_pair_count(key, part):
    return pair_tables(key)[1]


def shard_levels(stream_key, extent, cuts, low, high):
    def one(dim, shards_of):
        draws = jax.random.uniform(jax.random.fold_in(jax.random.fold_in(stream_key, 6), dim), (shards_of,), jnp.float32, low / len(cuts), high / len(cuts))
        return jnp.repeat(jnp.exp(draws), extent[dim] // shards_of).reshape((-1,) + (1,) * (len(extent) - dim - 1))

    level = one(*cuts[0])
    for cut in cuts[1:]:
        level = level * one(*cut)
    return level


def noise(stream_key, shape, width, bound, cuts=(), kind=jnp.bfloat16):
    array = width * jax.random.normal(stream_key, shape, jnp.float32)
    if cuts:
        array = array * shard_levels(stream_key, shape, cuts, -0.22, 0.18)
    return jnp.clip(array, -bound, bound).astype(kind)


def setup_inputs(seed: int = 0, part: int = 0) -> dict:
    keys = jax.random.split(jax.random.key(seed), 5)
    own_keys = jax.random.split(jax.random.fold_in(keys[4], part), 5)
    return {
        "traces": noise(own_keys[0], (NT, NP), 1.0, 6.0, ((0, 4), (1, 4)), jnp.float32),
        "centroids": jnp.clip(jax.random.uniform(own_keys[1], (3, NP), jnp.float32, -1.0, 1.0) * shard_levels(own_keys[1], (3, NP), ((1, 4),), -0.4, 0.0), -1.0, 1.0),
        "near_list": draw_near_list(jax.random.fold_in(jax.random.fold_in(keys[4], part), 71), part),
        "pair_count": draw_pair_count(jax.random.fold_in(jax.random.fold_in(keys[4], part), 71), part),
    }


damping = 0.999
time_step = 0.5
core_square = 0.01
highest = lax.Precision.HIGHEST

def forward_tables(times, freqs):
    product = freqs[:, None] * times[None, :] % NT
    angle = 2.0 * math.pi / NT * product.astype(jnp.float32)
    decay = jnp.exp(times.astype(jnp.float32) * math.log(damping))
    return (jnp.cos(angle) * decay[None, :], -jnp.sin(angle) * decay[None, :])

def inverse_tables(times, freqs):
    product = times[:, None] * freqs[None, :] % NT
    angle = 2.0 * math.pi / NT * product.astype(jnp.float32)
    growth = jnp.exp(-times.astype(jnp.float32) * math.log(damping)) / NT
    weight = jnp.where(freqs == 0, 1.0, 2.0).astype(jnp.float32)
    scale = growth[:, None] * weight[None, :]
    return (jnp.cos(angle) * scale, jnp.sin(angle) * scale)

def laplace(freqs):
    angle = 2.0 * math.pi / NT * freqs.astype(jnp.float32)
    return ((1.0 - damping * jnp.cos(angle)) / time_step, damping * jnp.sin(angle) / time_step)

def block_kernel(rows_xyz, cols_xyz, lap_re, lap_im):
    diff = rows_xyz[:, :, None] - cols_xyz[:, None, :]
    dist = jnp.sqrt(lax.optimization_barrier(jnp.sum(diff * diff, axis=0)) + core_square)
    decay = jnp.exp(-lap_re[:, None, None] * dist[None]) / (4.0 * math.pi * dist[None])
    phase = lap_im[:, None, None] * dist[None]
    return (decay * jnp.cos(phase), -decay * jnp.sin(phase))

def apply_pairs(ext_re, ext_im, ext_xyz, shard_list, count, lap_re, lap_im):
    kcount = ext_re.shape[0]
    own = ext_re.shape[1] - 2 * BLK

    def add_pair(slot, acc):
        acc_re, acc_im = acc
        row = shard_list[slot, 0].astype(jnp.int32)
        col = shard_list[slot, 1].astype(jnp.int32)
        rows_xyz = lax.dynamic_slice_in_dim(ext_xyz, (row + 1) * BLK, BLK, 1)
        cols_xyz = lax.dynamic_slice_in_dim(ext_xyz, col * BLK, BLK, 1)
        g_re = lax.dynamic_slice_in_dim(ext_re, col * BLK, BLK, 1)
        g_im = lax.dynamic_slice_in_dim(ext_im, col * BLK, BLK, 1)
        k_re, k_im = block_kernel(rows_xyz, cols_xyz, lap_re, lap_im)
        new_re = jnp.einsum('kij,kj->ki', k_re, g_re, precision=highest) - jnp.einsum('kij,kj->ki', k_im, g_im, precision=highest)
        new_im = jnp.einsum('kij,kj->ki', k_re, g_im, precision=highest) + jnp.einsum('kij,kj->ki', k_im, g_re, precision=highest)
        start = row * BLK
        acc_re = lax.dynamic_update_slice_in_dim(acc_re, lax.dynamic_slice_in_dim(acc_re, start, BLK, 1) + new_re, start, 1)
        acc_im = lax.dynamic_update_slice_in_dim(acc_im, lax.dynamic_slice_in_dim(acc_im, start, BLK, 1) + new_im, start, 1)
        return (acc_re, acc_im)
    zeros = jnp.zeros((kcount, own), jnp.float32)
    return lax.fori_loop(jnp.int32(0), count.astype(jnp.int32), add_pair, (zeros, zeros))

def reference(traces, centroids, near_list, pair_count):
    times = jnp.arange(NT, dtype=jnp.int32)
    freqs = jnp.arange(KH, dtype=jnp.int32)
    fcos, fsin = forward_tables(times, freqs)
    spec_re = jnp.dot(fcos, traces, precision=highest)
    spec_im = jnp.dot(fsin, traces, precision=highest)
    lap_re, lap_im = laplace(freqs)
    ext_index = (jnp.arange(N_PANEL, dtype=jnp.int32)[:, None] * PD - BLK + jnp.arange(PD + 2 * BLK, dtype=jnp.int32)[None, :]) % NP

    def shard_apply(shard):
        cols = ext_index[shard]
        return apply_pairs(spec_re[:, cols], spec_im[:, cols], centroids[:, cols], near_list[shard], pair_count[shard], lap_re, lap_im)
    out_re, out_im = lax.map(shard_apply, jnp.arange(N_PANEL, dtype=jnp.int32))
    out_re = jnp.transpose(out_re, (1, 0, 2)).reshape(KH, NP)
    out_im = jnp.transpose(out_im, (1, 0, 2)).reshape(KH, NP)
    icos, isin = inverse_tables(times, freqs)
    return jnp.dot(icos, out_re, precision=highest) - jnp.dot(isin, out_im, precision=highest)
```

```python
import math

import jax
import jax.numpy as jnp
from jax import lax
from jax.experimental import pallas as pl
from jax.experimental.pallas import tpu as pltpu
from jax.sharding import PartitionSpec as P

NT = 1024
BLK = 128
TAPS = 32
HALF = TAPS // 2
GEO = 8

damping = 0.999
time_step = 0.5
core_square = 0.01


def split(v):
    hi = v.astype(jnp.bfloat16)
    return hi, (v - hi.astype(jnp.float32)).astype(jnp.bfloat16)


def near_field(list_ref, count_ref, slab_ref, ext_ref, out_ref, shifted, coeffs, turned, acc, last):
    steps = out_ref.shape[0]
    blocks = acc.shape[0]
    geo = TAPS + steps
    for c in range(blocks + 2):
        for n in range(HALF):
            hi, lo = split(ext_ref[c, HALF - n : HALF - n + steps + HALF, :])
            shifted[c, 0, :, n * BLK : (n + 1) * BLK] = hi
            shifted[c, 1, :, n * BLK : (n + 1) * BLK] = lo
        rows = ext_ref[c, geo : geo + GEO, :]
        turned[c] = jnp.concatenate([rows] * (BLK // GEO), axis=0).T
    acc[...] = jnp.zeros_like(acc)
    last[...] = jnp.zeros_like(last)

    def add_pair(slot, carry):
        row = list_ref[slot, 0]
        col = list_ref[slot, 1]
        mine = ext_ref[row + 1, geo : geo + GEO, :]
        theirs = turned[col]
        square = jnp.full((BLK, BLK), core_square, jnp.float32)
        for a in range(3):
            diff = theirs[:, a : a + 1] - mine[a : a + 1, :]
            square = square + diff * diff
        dist = jnp.sqrt(square)
        x = dist * (1.0 / time_step)
        term = jnp.exp(-x) / (4.0 * math.pi * dist)
        nyquist = term * jnp.exp(-damping * x) * theirs[:, 3:4]
        last[row] = last[row] + jnp.sum(nyquist, axis=0, keepdims=True)
        for n in range(TAPS):
            hi, lo = split(term)
            coeffs[n * BLK : (n + 1) * BLK, :BLK] = hi
            coeffs[n * BLK : (n + 1) * BLK, BLK:] = lo
            term = term * (x * (1.0 / (n + 1)))
        near = coeffs[: HALF * BLK, :]
        far = coeffs[HALF * BLK :, :]
        total = acc[row]
        for part in range(2):
            both = jnp.dot(
                shifted[col, part, HALF:, :], near, preferred_element_type=jnp.float32
            ) + jnp.dot(
                shifted[col, part, :steps, :], far, preferred_element_type=jnp.float32
            )
            total = total + (both[:, :BLK] + both[:, BLK:])
        acc[row] = total
        return carry

    lax.fori_loop(0, count_ref[0], add_pair, 0)
    local = lax.broadcasted_iota(jnp.int32, (steps, BLK), 0)
    times = (slab_ref[0] * steps + local).astype(jnp.float32)
    growth = jnp.exp(-times * math.log(damping)) / NT
    growth = jnp.where(local % 2 == 0, growth, -growth)
    for r in range(blocks):
        out_ref[:, r * BLK : (r + 1) * BLK] = acc[r] - growth * last[r, 0:1, :]


def per_device(traces, centroids, near_list, pair_count):
    steps, width = traces.shape
    blocks = width // BLK
    groups = lax.axis_size("freq")
    shards = lax.axis_size("panel")
    position = lax.axis_index("freq")
    halo = lax.ppermute(
        traces[steps - TAPS :], "freq", [(i, (i + 1) % groups) for i in range(groups)]
    )
    halo = halo * jnp.where(position == 0, math.exp(NT * math.log(damping)), 1.0)
    times = position * steps + jnp.arange(steps, dtype=jnp.int32)
    weight = jnp.exp(times.astype(jnp.float32) * math.log(damping))
    weight = jnp.where(times % 2 == 0, weight, -weight)
    nyquist = lax.psum(jnp.sum(weight[:, None] * traces, axis=0, keepdims=True), "freq")
    pad = jnp.zeros((GEO - 4, width), jnp.float32)
    own = jnp.concatenate([halo, traces, centroids, nyquist, pad], axis=0)
    up = [(i, (i + 1) % shards) for i in range(shards)]
    before = lax.ppermute(own[:, width - BLK :], "panel", up)
    after = lax.ppermute(own[:, :BLK], "panel", [(j, i) for i, j in up])
    pieces = [before] + [own[:, r * BLK : (r + 1) * BLK] for r in range(blocks)] + [after]
    ext = jnp.stack(pieces, axis=0)
    smem = pl.BlockSpec(memory_space=pltpu.SMEM)
    return pl.pallas_call(
        near_field,
        out_shape=jax.ShapeDtypeStruct((steps, width), jnp.float32),
        in_specs=[smem, smem, smem, pl.BlockSpec(memory_space=pltpu.VMEM)],
        out_specs=pl.BlockSpec(memory_space=pltpu.VMEM),
        scratch_shapes=[
            pltpu.VMEM((blocks + 2, 2, steps + HALF, HALF * BLK), jnp.bfloat16),
            pltpu.VMEM((TAPS * BLK, 2 * BLK), jnp.bfloat16),
            pltpu.VMEM((blocks + 2, BLK, BLK), jnp.float32),
            pltpu.VMEM((blocks, steps, BLK), jnp.float32),
            pltpu.VMEM((blocks, 8, BLK), jnp.float32),
        ],
        compiler_params=pltpu.CompilerParams(vmem_limit_bytes=40 * 1024 * 1024),
    )(near_list[0], pair_count, position.reshape(1).astype(jnp.int32), ext)


def solution(mesh):
    in_specs = (
        P("freq", ("grp", "panel")),
        P(None, ("grp", "panel")),
        P(("grp", "panel"), None, None),
        P(("grp", "panel")),
    )
    out_specs = P("freq", ("grp", "panel"))
    return jax.shard_map(
        per_device, mesh=mesh, in_specs=in_specs, out_specs=out_specs, check_vma=False
    )
```

```python
import math

import jax
import jax.numpy as jnp
from jax import lax
from jax.experimental import pallas as pl
from jax.experimental.pallas import tpu as pltpu
from jax.sharding import PartitionSpec as P

NT = 1024
BLK = 128
TAPS = 32
HALF = TAPS // 2
GEO = 8

damping = 0.999
time_step = 0.5
core_square = 0.01


def split(v):
    hi = v.astype(jnp.bfloat16)
    return hi, (v - hi.astype(jnp.float32)).astype(jnp.bfloat16)


def near_field(
    list_ref, count_ref, slab_ref, ext_ref, nyquist_ref, out_ref, shifted, coeffs, turned, acc, last
):
    steps = out_ref.shape[0]
    blocks = acc.shape[0]
    geo = TAPS + steps
    for c in range(blocks + 2):
        for n in range(HALF):
            hi, lo = split(ext_ref[c, HALF - n : HALF - n + steps + HALF, :])
            shifted[c, 0, :, n * BLK : (n + 1) * BLK] = hi
            shifted[c, 1, :, n * BLK : (n + 1) * BLK] = lo
        place = lax.broadcasted_iota(jnp.int32, (GEO, BLK), 0)
        sample = jnp.sum(nyquist_ref[c], axis=0, keepdims=True)
        rows = jnp.where(place == 3, sample, ext_ref[c, geo : geo + GEO, :])
        turned[c] = jnp.concatenate([rows] * (BLK // GEO), axis=0).T
    acc[...] = jnp.zeros_like(acc)
    last[...] = jnp.zeros_like(last)

    def add_pair(slot, carry):
        row = list_ref[slot, 0]
        col = list_ref[slot, 1]
        mine = ext_ref[row + 1, geo : geo + GEO, :]
        theirs = turned[col]
        square = jnp.full((BLK, BLK), core_square, jnp.float32)
        for a in range(3):
            diff = theirs[:, a : a + 1] - mine[a : a + 1, :]
            square = square + diff * diff
        dist = jnp.sqrt(square)
        x = dist * (1.0 / time_step)
        term = jnp.exp(-x) / (4.0 * math.pi * dist)
        nyquist = term * jnp.exp(-damping * x) * theirs[:, 3:4]
        last[row] = last[row] + jnp.sum(nyquist, axis=0, keepdims=True)
        for n in range(TAPS):
            hi, lo = split(term)
            coeffs[n * BLK : (n + 1) * BLK, :BLK] = hi
            coeffs[n * BLK : (n + 1) * BLK, BLK:] = lo
            term = term * (x * (1.0 / (n + 1)))
        near = coeffs[: HALF * BLK, :]
        far = coeffs[HALF * BLK :, :]
        total = acc[row]
        for part in range(2):
            both = jnp.dot(
                shifted[col, part, HALF:, :], near, preferred_element_type=jnp.float32
            ) + jnp.dot(
                shifted[col, part, :steps, :], far, preferred_element_type=jnp.float32
            )
            total = total + (both[:, :BLK] + both[:, BLK:])
        acc[row] = total
        return carry

    lax.fori_loop(0, count_ref[0], add_pair, 0)
    local = lax.broadcasted_iota(jnp.int32, (steps, BLK), 0)
    times = (slab_ref[0] * steps + local).astype(jnp.float32)
    growth = jnp.exp(-times * math.log(damping)) / NT
    growth = jnp.where(local % 2 == 0, growth, -growth)
    for r in range(blocks):
        out_ref[:, r * BLK : (r + 1) * BLK] = acc[r] - growth * last[r, 0:1, :]


def exchange(traces_ref, xyz_ref, ext_ref, nyquist_ref, parts, slots, send, recv):
    steps, width = traces_ref.shape
    blocks = width // BLK
    geo = TAPS + steps
    groups = lax.axis_size("freq")
    shards = lax.axis_size("panel")
    position = lax.axis_index("freq")
    shard = lax.axis_index("panel")

    def device(ahead, side):
        return {
            "freq": lax.rem(position + ahead, groups),
            "panel": lax.rem(shard + side + shards, shards),
        }

    peers = [(s, d) for s in range(groups) for d in (0, 1, -1) if s or d]
    barrier = pltpu.get_barrier_semaphore()
    for s, d in peers:
        pl.semaphore_signal(
            barrier, inc=1, device_id=device(s, d), device_id_type=pl.DeviceIdType.MESH
        )
    times = position * steps + lax.broadcasted_iota(jnp.int32, (steps, BLK), 0)
    weight = jnp.exp(times.astype(jnp.float32) * math.log(damping))
    weight = jnp.where(times % 2 == 0, weight, -weight)
    for b in range(blocks):
        lanes = slice(b * BLK, (b + 1) * BLK)
        own = traces_ref[:, lanes]
        ext_ref[b + 1, TAPS:geo, :] = own
        ext_ref[b + 1, geo : geo + 3, :] = xyz_ref[:, lanes]
        ext_ref[b + 1, geo + 3 : geo + GEO, :] = jnp.zeros((GEO - 3, BLK), jnp.float32)
        parts[b] = jnp.sum((weight * own).reshape(steps // 8, 8, BLK), axis=0)
    pl.semaphore_wait(barrier, len(peers))
    inner = pl.ds(TAPS, steps + GEO)
    tail = pl.ds(steps, TAPS)
    head = pl.ds(0, TAPS)
    middle = pl.ds(1, blocks)
    moves = [
        (0, 1, ext_ref.at[blocks, inner], ext_ref.at[0, inner]),
        (0, -1, ext_ref.at[1, inner], ext_ref.at[blocks + 1, inner]),
        (1, 0, ext_ref.at[middle, tail], ext_ref.at[middle, head]),
        (1, 1, ext_ref.at[blocks, tail], ext_ref.at[0, head]),
        (1, -1, ext_ref.at[1, tail], ext_ref.at[blocks + 1, head]),
    ]
    for s, d in peers:
        if d == 0:
            moves.append((s, d, parts, slots.at[s, middle]))
        elif d == 1:
            moves.append((s, d, parts.at[blocks - 1], slots.at[s, 0]))
        else:
            moves.append((s, d, parts.at[0], slots.at[s, blocks + 1]))
    copies = []
    for i, (s, d, source, target) in enumerate(moves):
        copy = pltpu.make_async_remote_copy(
            src_ref=source,
            dst_ref=target,
            send_sem=send.at[i],
            recv_sem=recv.at[i],
            device_id=device(s, d),
            device_id_type=pl.DeviceIdType.MESH,
        )
        copy.start()
        copies.append(copy)
    for copy in copies:
        copy.wait()
    around = jnp.where(position == 0, math.exp(NT * math.log(damping)), 1.0)
    for c in range(blocks + 2):
        ext_ref[c, :TAPS, :] = ext_ref[c, :TAPS, :] * around
        total = parts[c - 1] if 1 <= c <= blocks else slots[0, c]
        for s in range(1, groups):
            total = total + slots[s, c]
        nyquist_ref[c] = total


def per_device(traces, centroids, near_list, pair_count):
    steps, width = traces.shape
    blocks = width // BLK
    groups = lax.axis_size("freq")
    position = lax.axis_index("freq")
    count = 5 + 3 * groups - 1
    vmem = pl.BlockSpec(memory_space=pltpu.VMEM)
    smem = pl.BlockSpec(memory_space=pltpu.SMEM)
    ext, nyquist = pl.pallas_call(
        exchange,
        out_shape=(
            jax.ShapeDtypeStruct((blocks + 2, TAPS + steps + GEO, BLK), jnp.float32),
            jax.ShapeDtypeStruct((blocks + 2, 8, BLK), jnp.float32),
        ),
        in_specs=[vmem, vmem],
        out_specs=(vmem, vmem),
        scratch_shapes=[
            pltpu.VMEM((blocks, 8, BLK), jnp.float32),
            pltpu.VMEM((groups, blocks + 2, 8, BLK), jnp.float32),
            pltpu.SemaphoreType.DMA((count,)),
            pltpu.SemaphoreType.DMA((count,)),
        ],
        compiler_params=pltpu.CompilerParams(collective_id=0, has_side_effects=True),
    )(traces, centroids)
    return pl.pallas_call(
        near_field,
        out_shape=jax.ShapeDtypeStruct((steps, width), jnp.float32),
        in_specs=[smem, smem, smem, vmem, vmem],
        out_specs=vmem,
        scratch_shapes=[
            pltpu.VMEM((blocks + 2, 2, steps + HALF, HALF * BLK), jnp.bfloat16),
            pltpu.VMEM((TAPS * BLK, 2 * BLK), jnp.bfloat16),
            pltpu.VMEM((blocks + 2, BLK, BLK), jnp.float32),
            pltpu.VMEM((blocks, steps, BLK), jnp.float32),
            pltpu.VMEM((blocks, 8, BLK), jnp.float32),
        ],
        compiler_params=pltpu.CompilerParams(vmem_limit_bytes=40 * 1024 * 1024),
    )(near_list[0], pair_count, position.reshape(1).astype(jnp.int32), ext, nyquist)


def solution(mesh):
    in_specs = (
        P("freq", ("grp", "panel")),
        P(None, ("grp", "panel")),
        P(("grp", "panel"), None, None),
        P(("grp", "panel")),
    )
    out_specs = P("freq", ("grp", "panel"))
    return jax.shard_map(
        per_device, mesh=mesh, in_specs=in_specs, out_specs=out_specs, check_vma=False
    )
```

```python
import math

import jax
import jax.numpy as jnp
from jax import lax
from jax.experimental import pallas as pl
from jax.experimental.pallas import tpu as pltpu
from jax.sharding import PartitionSpec as P

NT = 1024
BLK = 128
TAPS = 32
HALF = TAPS // 2
GEO = 8

damping = 0.999
time_step = 0.5
core_square = 0.01


def split(v):
    hi = v.astype(jnp.bfloat16)
    return hi, (v - hi.astype(jnp.float32)).astype(jnp.bfloat16)


def shift(shifted, ext, c, first, rows):
    for n in range(HALF):
        hi, lo = split(ext[c, first + HALF - n : first + HALF - n + rows, :])
        shifted[c, 0, first : first + rows, n * BLK : (n + 1) * BLK] = hi
        shifted[c, 1, first : first + rows, n * BLK : (n + 1) * BLK] = lo


def turn(geometry):
    return jnp.concatenate([geometry] * (BLK // GEO), axis=0).T


def contract(shifted, coeffs, col, steps):
    total = None
    for part in range(2):
        both = jnp.dot(
            shifted[col, part, HALF:, : HALF * BLK],
            coeffs[: HALF * BLK, :],
            preferred_element_type=jnp.float32,
        ) + jnp.dot(
            shifted[col, part, :steps, :],
            coeffs[HALF * BLK :, :],
            preferred_element_type=jnp.float32,
        )
        both = both[:, :BLK] + both[:, BLK:]
        total = both if total is None else total + both
    return total


def fill(coeffs, theirs, mine):
    square = jnp.full((BLK, BLK), core_square, jnp.float32)
    for a in range(3):
        diff = theirs[:, a : a + 1] - mine[a : a + 1, :]
        square = square + diff * diff
    dist = jnp.sqrt(square)
    x = dist * (1.0 / time_step)
    term = jnp.exp(-x) / (4.0 * math.pi * dist)

    def put(n, value):
        hi, lo = split(value)
        coeffs[n * BLK : (n + 1) * BLK, :BLK] = hi
        coeffs[n * BLK : (n + 1) * BLK, BLK:] = lo

    put(TAPS, term * jnp.exp(-damping * x))
    for n in range(TAPS):
        put(n, term)
        term = term * (x * (1.0 / (n + 1)))


def operator(
    list_ref,
    count_ref,
    traces_ref,
    xyz_ref,
    out_ref,
    ext_ref,
    shifted,
    even,
    odd,
    turned,
    acc,
    parts,
    slots,
    send,
    recv,
):
    steps, width = traces_ref.shape
    blocks = width // BLK
    geo = TAPS + steps
    groups = lax.axis_size("freq")
    shards = lax.axis_size("panel")
    position = lax.axis_index("freq")
    shard = lax.axis_index("panel")

    def device(ahead, side):
        return {
            "freq": lax.rem(position + ahead, groups),
            "panel": lax.rem(shard + side + shards, shards),
        }

    peers = [(s, d) for s in range(groups) for d in (0, 1, -1) if s or d]
    barrier = pltpu.get_barrier_semaphore()
    for s, d in peers:
        pl.semaphore_signal(
            barrier, inc=1, device_id=device(s, d), device_id_type=pl.DeviceIdType.MESH
        )
    times = position * steps + lax.broadcasted_iota(jnp.int32, (steps, BLK), 0)
    weight = jnp.exp(times.astype(jnp.float32) * math.log(damping))
    weight = jnp.where(times % 2 == 0, weight, -weight)
    for b in range(blocks):
        lanes = slice(b * BLK, (b + 1) * BLK)
        own = traces_ref[:, lanes]
        ext_ref[b + 1, TAPS:geo, :] = own
        ext_ref[b + 1, geo : geo + 3, :] = xyz_ref[:, lanes]
        ext_ref[b + 1, geo + 3 : geo + GEO, :] = jnp.zeros((GEO - 3, BLK), jnp.float32)
        parts[b] = jnp.sum((weight * own).reshape(steps // 8, 8, BLK), axis=0)
    pl.semaphore_wait(barrier, len(peers))
    inner = pl.ds(TAPS, steps + GEO)
    tail = pl.ds(steps, TAPS)
    head = pl.ds(0, TAPS)
    middle = pl.ds(1, blocks)
    moves = [
        (0, 1, ext_ref.at[blocks, inner], ext_ref.at[0, inner]),
        (0, -1, ext_ref.at[1, inner], ext_ref.at[blocks + 1, inner]),
        (1, 0, ext_ref.at[middle, tail], ext_ref.at[middle, head]),
        (1, 1, ext_ref.at[blocks, tail], ext_ref.at[0, head]),
        (1, -1, ext_ref.at[1, tail], ext_ref.at[blocks + 1, head]),
    ]
    for s, d in peers:
        if d == 0:
            moves.append((s, d, parts, slots.at[s, middle]))
        elif d == 1:
            moves.append((s, d, parts.at[blocks - 1], slots.at[s, 0]))
        else:
            moves.append((s, d, parts.at[0], slots.at[s, blocks + 1]))
    copies = []
    for i, (s, d, source, target) in enumerate(moves):
        copy = pltpu.make_async_remote_copy(
            src_ref=source,
            dst_ref=target,
            send_sem=send.at[i],
            recv_sem=recv.at[i],
            device_id=device(s, d),
            device_id_type=pl.DeviceIdType.MESH,
        )
        copy.start()
        copies.append(copy)
    for c in range(1, blocks + 1):
        turned[c] = turn(ext_ref[c, geo : geo + GEO, :])
    fill(even, turned[1], ext_ref[1, geo : geo + GEO, :])
    for c in range(1, blocks + 1):
        shift(shifted, ext_ref, c, TAPS, steps + HALF - TAPS)
    acc[...] = jnp.zeros_like(acc)
    local = lax.broadcasted_iota(jnp.int32, (steps, BLK), 0)
    growth = jnp.exp((position * steps + local).astype(jnp.float32) * -math.log(damping)) / NT
    growth = jnp.where(local % 2 == 0, -growth, growth)
    for copy in copies:
        copy.wait()
    around = jnp.where(position == 0, math.exp(NT * math.log(damping)), 1.0)
    for c in range(blocks + 2):
        ext_ref[c, :TAPS, :] = ext_ref[c, :TAPS, :] * around
        total = parts[c - 1] if 1 <= c <= blocks else slots[0, c]
        for s in range(1, groups):
            total = total + slots[s, c]
        hi, lo = split(growth * jnp.sum(total, axis=0, keepdims=True))
        shifted[c, 0, :steps, HALF * BLK :] = hi
        shifted[c, 1, :steps, HALF * BLK :] = lo
        if 1 <= c <= blocks:
            shift(shifted, ext_ref, c, 0, TAPS)
        else:
            shift(shifted, ext_ref, c, 0, steps + HALF)
            turned[c] = turn(ext_ref[c, geo : geo + GEO, :])
    pairs = list_ref.shape[0]

    def step(slot, now, later):
        following = jnp.minimum(slot + 1, pairs - 1)
        row = list_ref[following, 0]
        col = list_ref[following, 1]
        mine = ext_ref[row + 1, geo : geo + GEO, :]
        theirs = turned[col]
        total = contract(shifted, now, list_ref[slot, 1], steps)
        fill(later, theirs, mine)
        target = jnp.where(slot < count_ref[0], list_ref[slot, 0], blocks)
        for r in range(blocks):
            acc[r] = acc[r] + jnp.where(target == r, total, 0.0)

    def two(i, carry):
        step(2 * i, even, odd)
        step(2 * i + 1, odd, even)
        return carry

    lax.fori_loop(0, pairs // 2, two, 0)
    for r in range(blocks):
        out_ref[:, r * BLK : (r + 1) * BLK] = acc[r]


def per_device(traces, centroids, near_list, pair_count):
    steps, width = traces.shape
    blocks = width // BLK
    groups = lax.axis_size("freq")
    count = 5 + 3 * groups - 1
    depth = (TAPS + 1) * BLK
    vmem = pl.BlockSpec(memory_space=pltpu.VMEM)
    smem = pl.BlockSpec(memory_space=pltpu.SMEM)
    return pl.pallas_call(
        operator,
        out_shape=jax.ShapeDtypeStruct((steps, width), jnp.float32),
        in_specs=[smem, smem, vmem, vmem],
        out_specs=vmem,
        scratch_shapes=[
            pltpu.VMEM((blocks + 2, TAPS + steps + GEO, BLK), jnp.float32),
            pltpu.VMEM((blocks + 2, 2, steps + HALF, (HALF + 1) * BLK), jnp.bfloat16),
            pltpu.VMEM((depth, 2 * BLK), jnp.bfloat16),
            pltpu.VMEM((depth, 2 * BLK), jnp.bfloat16),
            pltpu.VMEM((blocks + 2, BLK, BLK), jnp.float32),
            pltpu.VMEM((blocks, steps, BLK), jnp.float32),
            pltpu.VMEM((blocks, 8, BLK), jnp.float32),
            pltpu.VMEM((groups, blocks + 2, 8, BLK), jnp.float32),
            pltpu.SemaphoreType.DMA((count,)),
            pltpu.SemaphoreType.DMA((count,)),
        ],
        compiler_params=pltpu.CompilerParams(
            collective_id=0, has_side_effects=True, vmem_limit_bytes=40 * 1024 * 1024
        ),
    )(near_list[0], pair_count, traces, centroids)


def solution(mesh):
    in_specs = (
        P("freq", ("grp", "panel")),
        P(None, ("grp", "panel")),
        P(("grp", "panel"), None, None),
        P(("grp", "panel")),
    )
    out_specs = P("freq", ("grp", "panel"))
    return jax.shard_map(
        per_device, mesh=mesh, in_specs=in_specs, out_specs=out_specs, check_vma=False
    )
```

```python
import math

import jax
import jax.numpy as jnp
from jax import lax
from jax.experimental import pallas as pl
from jax.experimental.pallas import tpu as pltpu
from jax.sharding import PartitionSpec as P

NT = 1024
BLK = 128
TAPS = 32
HALF = TAPS // 2
PAIR = HALF // 2
GEO = 8

damping = 0.999
time_step = 0.5
core_square = 0.01


def split(v):
    hi = v.astype(jnp.bfloat16)
    return hi, (v - hi.astype(jnp.float32)).astype(jnp.bfloat16)


def shift(high, low, ext, c, first, rows):
    for n in range(HALF):
        hi, lo = split(ext[c, first + HALF - n : first + HALF - n + rows, :])
        high[c, first : first + rows, n * BLK : (n + 1) * BLK] = hi
        if n < PAIR:
            low[c, first : first + rows, n * BLK : (n + 1) * BLK] = lo


def turn(geometry):
    return jnp.concatenate([geometry] * (BLK // GEO), axis=0).T


def product(x, y):
    return jnp.dot(x, y, preferred_element_type=jnp.float32)


def contract(high, low, coeffs, col, steps):
    rows = steps + HALF
    one, two, three = HALF * BLK, (HALF + PAIR) * BLK, (HALF + 2 * PAIR) * BLK
    both = product(high[col, HALF:, :], coeffs[:one, :])
    total = both[:, :BLK] + both[:, BLK:]
    cross = product(low[col], coeffs[one:two, :])
    total = total + (cross[HALF:rows, :BLK] + cross[HALF - PAIR : rows - PAIR, BLK:])
    far = product(high[col, :, PAIR * BLK :], coeffs[two:three, :])
    return total + (far[PAIR : PAIR + steps, :BLK] + far[:steps, BLK:])


def fill(coeffs, sample, theirs, mine):
    square = jnp.full((BLK, BLK), core_square, jnp.float32)
    for a in range(3):
        diff = theirs[:, a : a + 1] - mine[a : a + 1, :]
        square = square + diff * diff
    dist = jnp.sqrt(square)
    x = dist * (1.0 / time_step)
    term = jnp.exp(-x) / (4.0 * math.pi * dist)
    sample[...] = term * jnp.exp(-damping * x)

    def put(place, half, value):
        coeffs[place * BLK : (place + 1) * BLK, half * BLK : (half + 1) * BLK] = value

    for n in range(TAPS):
        if n < HALF:
            hi, lo = split(term)
            put(n, 0, hi)
            put(n, 1, lo)
        else:
            hi = term.astype(jnp.bfloat16)
        put(HALF + n // HALF * PAIR + n % PAIR, n // PAIR % 2, hi)
        term = term * (x * (1.0 / (n + 1)))


def operator(
    list_ref,
    count_ref,
    traces_ref,
    xyz_ref,
    out_ref,
    ext_ref,
    high,
    low,
    even,
    odd,
    even_sample,
    odd_sample,
    turned,
    acc,
    last,
    parts,
    slots,
    send,
    recv,
    load,
):
    steps, width = traces_ref.shape
    blocks = width // BLK
    geo = TAPS + steps
    groups = lax.axis_size("freq")
    shards = lax.axis_size("panel")
    position = lax.axis_index("freq")
    shard = lax.axis_index("panel")

    def device(ahead, side):
        return {
            "freq": lax.rem(position + ahead, groups),
            "panel": lax.rem(shard + side + shards, shards),
        }

    peers = [(s, d) for s in range(groups) for d in (0, 1, -1) if s or d]
    barrier = pltpu.get_barrier_semaphore()
    for s, d in peers:
        pl.semaphore_signal(
            barrier, inc=1, device_id=device(s, d), device_id_type=pl.DeviceIdType.MESH
        )
    loads = [
        pltpu.make_async_copy(
            traces_ref.at[:, pl.ds(b * BLK, BLK)],
            ext_ref.at[b + 1, pl.ds(TAPS, steps)],
            load.at[b],
        )
        for b in range(blocks)
    ]
    for copy in loads:
        copy.start()
    times = position * steps + lax.broadcasted_iota(jnp.int32, (steps, BLK), 0)
    weight = jnp.exp(times.astype(jnp.float32) * math.log(damping))
    weight = jnp.where(times % 2 == 0, weight, -weight)
    for b in range(blocks):
        lanes = slice(b * BLK, (b + 1) * BLK)
        ext_ref[b + 1, geo : geo + 3, :] = xyz_ref[:, lanes]
        ext_ref[b + 1, geo + 3 : geo + GEO, :] = jnp.zeros((GEO - 3, BLK), jnp.float32)
    for b in range(blocks):
        loads[b].wait()
        own = ext_ref[b + 1, TAPS:geo, :]
        parts[b] = jnp.sum((weight * own).reshape(steps // 8, 8, BLK), axis=0)
    pl.semaphore_wait(barrier, len(peers))
    inner = pl.ds(TAPS, steps + GEO)
    tail = pl.ds(steps, TAPS)
    head = pl.ds(0, TAPS)
    middle = pl.ds(1, blocks)
    moves = [
        (0, 1, ext_ref.at[blocks, inner], ext_ref.at[0, inner]),
        (0, -1, ext_ref.at[1, inner], ext_ref.at[blocks + 1, inner]),
        (1, 0, ext_ref.at[middle, tail], ext_ref.at[middle, head]),
        (1, 1, ext_ref.at[blocks, tail], ext_ref.at[0, head]),
        (1, -1, ext_ref.at[1, tail], ext_ref.at[blocks + 1, head]),
    ]
    for s, d in peers:
        if d == 0:
            moves.append((s, d, parts, slots.at[s, middle]))
        elif d == 1:
            moves.append((s, d, parts.at[blocks - 1], slots.at[s, 0]))
        else:
            moves.append((s, d, parts.at[0], slots.at[s, blocks + 1]))
    copies = []
    for i, (s, d, source, target) in enumerate(moves):
        copy = pltpu.make_async_remote_copy(
            src_ref=source,
            dst_ref=target,
            send_sem=send.at[i],
            recv_sem=recv.at[i],
            device_id=device(s, d),
            device_id_type=pl.DeviceIdType.MESH,
        )
        copy.start()
        copies.append(copy)
    for c in range(1, blocks + 1):
        turned[c] = turn(ext_ref[c, geo : geo + GEO, :])
    fill(even, even_sample, turned[1], ext_ref[1, geo : geo + GEO, :])
    for c in range(1, blocks + 1):
        shift(high, low, ext_ref, c, TAPS, steps + HALF - TAPS)
    acc[...] = jnp.zeros_like(acc)
    last[...] = jnp.zeros_like(last)
    local = lax.broadcasted_iota(jnp.int32, (steps, BLK), 0)
    growth = jnp.exp((position * steps + local).astype(jnp.float32) * -math.log(damping)) / NT
    growth = jnp.where(local % 2 == 0, -growth, growth)
    for copy in copies:
        copy.wait()
    around = jnp.where(position == 0, math.exp(NT * math.log(damping)), 1.0)
    for c in range(blocks + 2):
        ext_ref[c, :TAPS, :] = ext_ref[c, :TAPS, :] * around
        total = parts[c - 1] if 1 <= c <= blocks else slots[0, c]
        for s in range(1, groups):
            total = total + slots[s, c]
        place = lax.broadcasted_iota(jnp.int32, (GEO, BLK), 0)
        total = jnp.sum(total, axis=0, keepdims=True)
        turned[c] = turn(jnp.where(place == 3, total, ext_ref[c, geo : geo + GEO, :]))
        if 1 <= c <= blocks:
            shift(high, low, ext_ref, c, 0, TAPS)
        else:
            shift(high, low, ext_ref, c, 0, steps + HALF)
    pairs = list_ref.shape[1]

    def step(slot, now, now_sample, later, later_sample):
        following = jnp.minimum(slot + 1, pairs - 1)
        row = list_ref[0, following]
        col = list_ref[1, following]
        mine = ext_ref[row + 1, geo : geo + GEO, :]
        theirs = turned[col]
        col = list_ref[1, slot]
        total = contract(high, low, now, col, steps)
        sums = jnp.sum(now_sample[...] * turned[col][:, 3:4], axis=0, keepdims=True)
        fill(later, later_sample, theirs, mine)
        target = jnp.where(slot < count_ref[0], list_ref[0, slot], blocks)
        for r in range(blocks):
            acc[r] = acc[r] + jnp.where(target == r, total, 0.0)
            last[r] = last[r] + jnp.where(target == r, sums, 0.0)

    def two(i, carry):
        step(2 * i, even, even_sample, odd, odd_sample)
        step(2 * i + 1, odd, odd_sample, even, even_sample)
        return carry

    lax.fori_loop(0, pairs // 2, two, 0)
    for r in range(blocks):
        out_ref[:, r * BLK : (r + 1) * BLK] = acc[r] + growth * last[r, 0:1, :]


def per_device(traces, centroids, near_list, pair_count):
    steps, width = traces.shape
    blocks = width // BLK
    groups = lax.axis_size("freq")
    count = 5 + 3 * groups - 1
    depth = (HALF + 2 * PAIR) * BLK
    vmem = pl.BlockSpec(memory_space=pltpu.VMEM)
    smem = pl.BlockSpec(memory_space=pltpu.SMEM)
    return pl.pallas_call(
        operator,
        out_shape=jax.ShapeDtypeStruct((steps, width), jnp.float32),
        in_specs=[smem, smem, pl.BlockSpec(memory_space=pltpu.HBM), vmem],
        out_specs=vmem,
        scratch_shapes=[
            pltpu.VMEM((blocks + 2, TAPS + steps + GEO, BLK), jnp.float32),
            pltpu.VMEM((blocks + 2, steps + HALF, HALF * BLK), jnp.bfloat16),
            pltpu.VMEM((blocks + 2, steps + HALF, PAIR * BLK), jnp.bfloat16),
            pltpu.VMEM((depth, 2 * BLK), jnp.bfloat16),
            pltpu.VMEM((depth, 2 * BLK), jnp.bfloat16),
            pltpu.VMEM((BLK, BLK), jnp.float32),
            pltpu.VMEM((BLK, BLK), jnp.float32),
            pltpu.VMEM((blocks + 2, BLK, BLK), jnp.float32),
            pltpu.VMEM((blocks, steps, BLK), jnp.float32),
            pltpu.VMEM((blocks, 8, BLK), jnp.float32),
            pltpu.VMEM((blocks, 8, BLK), jnp.float32),
            pltpu.VMEM((groups, blocks + 2, 8, BLK), jnp.float32),
            pltpu.SemaphoreType.DMA((count,)),
            pltpu.SemaphoreType.DMA((count,)),
            pltpu.SemaphoreType.DMA((blocks,)),
        ],
        compiler_params=pltpu.CompilerParams(
            collective_id=0, has_side_effects=True, vmem_limit_bytes=60 * 1024 * 1024
        ),
    )(near_list[0].T, pair_count, traces, centroids)


def solution(mesh):
    in_specs = (
        P("freq", ("grp", "panel")),
        P(None, ("grp", "panel")),
        P(("grp", "panel"), None, None),
        P(("grp", "panel")),
    )
    out_specs = P("freq", ("grp", "panel"))
    return jax.shard_map(
        per_device, mesh=mesh, in_specs=in_specs, out_specs=out_specs, check_vma=False
    )
```

```python
import math

import jax
import jax.numpy as jnp
from jax import lax
from jax.experimental import pallas as pl
from jax.experimental.pallas import tpu as pltpu
from jax.sharding import PartitionSpec as P

NT = 1024
BLK = 128
TAPS = 32
HALF = TAPS // 2
PAIR = HALF // 2
GEO = 8

damping = 0.999
time_step = 0.5
core_square = 0.01


def split(v):
    hi = v.astype(jnp.bfloat16)
    return hi, (v - hi.astype(jnp.float32)).astype(jnp.bfloat16)


def shift(high, low, ext, c, first, rows):
    for n in range(HALF):
        hi, lo = split(ext[c, first + HALF - n : first + HALF - n + rows, :])
        high[c, first : first + rows, n * BLK : (n + 1) * BLK] = hi
        if n < PAIR:
            low[c, first : first + rows, n * BLK : (n + 1) * BLK] = lo


def turn(geometry):
    return jnp.concatenate([geometry] * (BLK // GEO), axis=0).T


def product(x, y):
    return jnp.dot(x, y, preferred_element_type=jnp.float32)


def contract(high, low, coeffs, col, steps):
    rows = steps + HALF
    one, two, three = HALF * BLK, (HALF + PAIR) * BLK, (HALF + 2 * PAIR) * BLK
    both = product(high[col, HALF:, :], coeffs[:one, :])
    total = both[:, :BLK] + both[:, BLK:]
    cross = product(low[col], coeffs[one:two, :])
    total = total + (cross[HALF:rows, :BLK] + cross[HALF - PAIR : rows - PAIR, BLK:])
    far = product(high[col, :, PAIR * BLK :], coeffs[two:three, :])
    return total + (far[PAIR : PAIR + steps, :BLK] + far[:steps, BLK:])


def fill(coeffs, sample, theirs, mine):
    square = jnp.full((BLK, BLK), core_square, jnp.float32)
    for a in range(3):
        diff = theirs[:, a : a + 1] - mine[a : a + 1, :]
        square = square + diff * diff
    dist = jnp.sqrt(square)
    x = dist * (1.0 / time_step)
    term = jnp.exp(-x) / (4.0 * math.pi * dist)
    sample[...] = term * jnp.exp(-damping * x)

    def put(place, half, value):
        coeffs[place * BLK : (place + 1) * BLK, half * BLK : (half + 1) * BLK] = value

    for n in range(TAPS):
        if n < HALF:
            hi, lo = split(term)
            put(n, 0, hi)
            put(n, 1, lo)
        else:
            hi = term.astype(jnp.bfloat16)
        put(HALF + n // HALF * PAIR + n % PAIR, n // PAIR % 2, hi)
        term = term * (x * (1.0 / (n + 1)))


def operator(
    list_ref,
    count_ref,
    traces_ref,
    xyz_ref,
    out_ref,
    ext_ref,
    high,
    low,
    even,
    odd,
    even_sample,
    odd_sample,
    turned,
    acc,
    last,
    parts,
    slots,
    send,
    recv,
    load,
):
    steps, width = traces_ref.shape
    blocks = width // BLK
    geo = TAPS + steps
    groups = lax.axis_size("freq")
    shards = lax.axis_size("panel")
    position = lax.axis_index("freq")
    shard = lax.axis_index("panel")

    def device(ahead, side):
        return {
            "freq": lax.rem(position + ahead, groups),
            "panel": lax.rem(shard + side + shards, shards),
        }

    peers = [(s, d) for s in range(groups) for d in (0, 1, -1) if s or d]
    barrier = pltpu.get_barrier_semaphore()
    for s, d in peers:
        pl.semaphore_signal(
            barrier, inc=1, device_id=device(s, d), device_id_type=pl.DeviceIdType.MESH
        )
    loads = [
        pltpu.make_async_copy(
            traces_ref.at[:, pl.ds(b * BLK, BLK)],
            ext_ref.at[b + 1, pl.ds(TAPS, steps)],
            load.at[b],
        )
        for b in range(blocks)
    ]
    for copy in loads:
        copy.start()
    times = position * steps + lax.broadcasted_iota(jnp.int32, (steps, BLK), 0)
    weight = jnp.exp(times.astype(jnp.float32) * math.log(damping))
    weight = jnp.where(times % 2 == 0, weight, -weight)
    for b in range(blocks):
        lanes = slice(b * BLK, (b + 1) * BLK)
        ext_ref[b + 1, geo : geo + 3, :] = xyz_ref[:, lanes]
        ext_ref[b + 1, geo + 3 : geo + GEO, :] = jnp.zeros((GEO - 3, BLK), jnp.float32)
    for b in range(blocks):
        loads[b].wait()
        own = ext_ref[b + 1, TAPS:geo, :]
        parts[b] = jnp.sum((weight * own).reshape(steps // 8, 8, BLK), axis=0)
    turned[1] = turn(ext_ref[1, geo : geo + GEO, :])
    fill(even, even_sample, turned[1], ext_ref[1, geo : geo + GEO, :])
    pl.semaphore_wait(barrier, len(peers))
    inner = pl.ds(TAPS, steps + GEO)
    tail = pl.ds(steps, TAPS)
    head = pl.ds(0, TAPS)
    middle = pl.ds(1, blocks)
    moves = [
        (0, 1, ext_ref.at[blocks, inner], ext_ref.at[0, inner]),
        (0, -1, ext_ref.at[1, inner], ext_ref.at[blocks + 1, inner]),
        (1, 0, ext_ref.at[middle, tail], ext_ref.at[middle, head]),
        (1, 1, ext_ref.at[blocks, tail], ext_ref.at[0, head]),
        (1, -1, ext_ref.at[1, tail], ext_ref.at[blocks + 1, head]),
    ]
    for s, d in peers:
        if d == 0:
            moves.append((s, d, parts, slots.at[s, middle]))
        elif d == 1:
            moves.append((s, d, parts.at[blocks - 1], slots.at[s, 0]))
        else:
            moves.append((s, d, parts.at[0], slots.at[s, blocks + 1]))
    copies = []
    for i, (s, d, source, target) in enumerate(moves):
        copy = pltpu.make_async_remote_copy(
            src_ref=source,
            dst_ref=target,
            send_sem=send.at[i],
            recv_sem=recv.at[i],
            device_id=device(s, d),
            device_id_type=pl.DeviceIdType.MESH,
        )
        copy.start()
        copies.append(copy)
    for c in range(1, blocks + 1):
        shift(high, low, ext_ref, c, TAPS, steps + HALF - TAPS)
    acc[...] = jnp.zeros_like(acc)
    last[...] = jnp.zeros_like(last)
    local = lax.broadcasted_iota(jnp.int32, (steps, BLK), 0)
    growth = jnp.exp((position * steps + local).astype(jnp.float32) * -math.log(damping)) / NT
    growth = jnp.where(local % 2 == 0, -growth, growth)
    for copy, c in zip(copies[:2], (0, blocks + 1)):
        copy.wait()
        shift(high, low, ext_ref, c, TAPS, steps + HALF - TAPS)
    for copy in copies[2:]:
        copy.wait()
    around = jnp.where(position == 0, math.exp(NT * math.log(damping)), 1.0)
    for c in range(blocks + 2):
        ext_ref[c, :TAPS, :] = ext_ref[c, :TAPS, :] * around
        total = parts[c - 1] if 1 <= c <= blocks else slots[0, c]
        for s in range(1, groups):
            total = total + slots[s, c]
        place = lax.broadcasted_iota(jnp.int32, (GEO, BLK), 0)
        total = jnp.sum(total, axis=0, keepdims=True)
        turned[c] = turn(jnp.where(place == 3, total, ext_ref[c, geo : geo + GEO, :]))
        shift(high, low, ext_ref, c, 0, TAPS)
    pairs = list_ref.shape[1]

    def step(slot, now, now_sample, later, later_sample):
        following = jnp.minimum(slot + 1, pairs - 1)
        row = list_ref[0, following]
        col = list_ref[1, following]
        mine = ext_ref[row + 1, geo : geo + GEO, :]
        theirs = turned[col]
        col = list_ref[1, slot]
        total = contract(high, low, now, col, steps)
        sums = jnp.sum(now_sample[...] * turned[col][:, 3:4], axis=0, keepdims=True)
        fill(later, later_sample, theirs, mine)
        target = jnp.where(slot < count_ref[0], list_ref[0, slot], blocks)
        for r in range(blocks):
            acc[r] = acc[r] + jnp.where(target == r, total, 0.0)
            last[r] = last[r] + jnp.where(target == r, sums, 0.0)

    def two(i, carry):
        step(2 * i, even, even_sample, odd, odd_sample)
        step(2 * i + 1, odd, odd_sample, even, even_sample)
        return carry

    lax.fori_loop(0, pairs // 2, two, 0)
    for r in range(blocks):
        out_ref[:, r * BLK : (r + 1) * BLK] = acc[r] + growth * last[r, 0:1, :]


def per_device(traces, centroids, near_list, pair_count):
    steps, width = traces.shape
    blocks = width // BLK
    groups = lax.axis_size("freq")
    count = 5 + 3 * groups - 1
    depth = (HALF + 2 * PAIR) * BLK
    vmem = pl.BlockSpec(memory_space=pltpu.VMEM)
    smem = pl.BlockSpec(memory_space=pltpu.SMEM)
    return pl.pallas_call(
        operator,
        out_shape=jax.ShapeDtypeStruct((steps, width), jnp.float32),
        in_specs=[smem, smem, pl.BlockSpec(memory_space=pltpu.HBM), vmem],
        out_specs=vmem,
        scratch_shapes=[
            pltpu.VMEM((blocks + 2, TAPS + steps + GEO, BLK), jnp.float32),
            pltpu.VMEM((blocks + 2, steps + HALF, HALF * BLK), jnp.bfloat16),
            pltpu.VMEM((blocks + 2, steps + HALF, PAIR * BLK), jnp.bfloat16),
            pltpu.VMEM((depth, 2 * BLK), jnp.bfloat16),
            pltpu.VMEM((depth, 2 * BLK), jnp.bfloat16),
            pltpu.VMEM((BLK, BLK), jnp.float32),
            pltpu.VMEM((BLK, BLK), jnp.float32),
            pltpu.VMEM((blocks + 2, BLK, BLK), jnp.float32),
            pltpu.VMEM((blocks, steps, BLK), jnp.float32),
            pltpu.VMEM((blocks, 8, BLK), jnp.float32),
            pltpu.VMEM((blocks, 8, BLK), jnp.float32),
            pltpu.VMEM((groups, blocks + 2, 8, BLK), jnp.float32),
            pltpu.SemaphoreType.DMA((count,)),
            pltpu.SemaphoreType.DMA((count,)),
            pltpu.SemaphoreType.DMA((blocks,)),
        ],
        compiler_params=pltpu.CompilerParams(
            collective_id=0, has_side_effects=True, vmem_limit_bytes=60 * 1024 * 1024
        ),
    )(near_list[0].T, pair_count, traces, centroids)


def solution(mesh):
    in_specs = (
        P("freq", ("grp", "panel")),
        P(None, ("grp", "panel")),
        P(("grp", "panel"), None, None),
        P(("grp", "panel")),
    )
    out_specs = P("freq", ("grp", "panel"))
    return jax.shard_map(
        per_device, mesh=mesh, in_specs=in_specs, out_specs=out_specs, check_vma=False
    )
```

```python
import math

import jax
import jax.numpy as jnp
from jax import lax
from jax.experimental import pallas as pl
from jax.experimental.pallas import tpu as pltpu
from jax.sharding import PartitionSpec as P

NT = 1024
BLK = 128
TAPS = 32
HALF = TAPS // 2
PAIR = HALF // 2
GEO = 8

damping = 0.999
time_step = 0.5
core_square = 0.01


def split(v):
    hi = v.astype(jnp.bfloat16)
    return hi, (v - hi.astype(jnp.float32)).astype(jnp.bfloat16)


def shift(high, low, ext, c, first, rows):
    for n in range(HALF):
        hi, lo = split(ext[c, first + HALF - n : first + HALF - n + rows, :])
        high[c, first : first + rows, n * BLK : (n + 1) * BLK] = hi
        if n < PAIR:
            low[c, first : first + rows, n * BLK : (n + 1) * BLK] = lo


def turn(geometry):
    return jnp.concatenate([geometry] * (BLK // GEO), axis=0).T


def product(x, y):
    return jnp.dot(x, y, preferred_element_type=jnp.float32)


def contract(high, low, coeffs, col, steps):
    rows = steps + HALF
    one, two, three = HALF * BLK, (HALF + PAIR) * BLK, (HALF + 2 * PAIR) * BLK
    both = product(high[col, HALF:, :], coeffs[:one, :])
    total = both[:, :BLK] + both[:, BLK:]
    cross = product(low[col], coeffs[one:two, :])
    total = total + (cross[HALF:rows, :BLK] + cross[HALF - PAIR : rows - PAIR, BLK:])
    far = product(high[col, :, PAIR * BLK :], coeffs[two:three, :])
    return total + (far[PAIR : PAIR + steps, :BLK] + far[:steps, BLK:])


def fill(coeffs, sample, theirs, mine):
    square = jnp.full((BLK, BLK), core_square, jnp.float32)
    for a in range(3):
        diff = theirs[:, a : a + 1] - mine[a : a + 1, :]
        square = square + diff * diff
    dist = jnp.sqrt(square)
    x = dist * (1.0 / time_step)
    term = jnp.exp(-x) / (4.0 * math.pi * dist)
    sample[...] = term * jnp.exp(-damping * x)

    def put(place, half, value):
        coeffs[place * BLK : (place + 1) * BLK, half * BLK : (half + 1) * BLK] = value

    for n in range(TAPS):
        if n < HALF:
            hi, lo = split(term)
            put(n, 0, hi)
            put(n, 1, lo)
        else:
            hi = term.astype(jnp.bfloat16)
        put(HALF + n // HALF * PAIR + n % PAIR, n // PAIR % 2, hi)
        term = term * (x * (1.0 / (n + 1)))


def operator(
    list_ref,
    count_ref,
    traces_ref,
    xyz_ref,
    out_ref,
    ext_ref,
    high,
    low,
    even,
    odd,
    even_sample,
    odd_sample,
    turned,
    acc,
    last,
    parts,
    slots,
    send,
    recv,
    load,
):
    steps, width = traces_ref.shape
    blocks = width // BLK
    geo = TAPS + steps
    groups = lax.axis_size("freq")
    shards = lax.axis_size("panel")
    position = lax.axis_index("freq")
    shard = lax.axis_index("panel")

    def device(ahead, side):
        return {
            "freq": lax.rem(position + ahead, groups),
            "panel": lax.rem(shard + side + shards, shards),
        }

    peers = [(s, d) for s in range(groups) for d in (0, 1, -1) if s or d]
    barrier = pltpu.get_barrier_semaphore()
    for s, d in peers:
        pl.semaphore_signal(
            barrier, inc=1, device_id=device(s, d), device_id_type=pl.DeviceIdType.MESH
        )
    loads = [
        pltpu.make_async_copy(
            traces_ref.at[:, pl.ds(b * BLK, BLK)],
            ext_ref.at[b + 1, pl.ds(TAPS, steps)],
            load.at[b],
        )
        for b in range(blocks)
    ]
    for copy in loads:
        copy.start()
    times = position * steps + lax.broadcasted_iota(jnp.int32, (steps, BLK), 0)
    weight = jnp.exp(times.astype(jnp.float32) * math.log(damping))
    weight = jnp.where(times % 2 == 0, weight, -weight)
    for b in range(blocks):
        lanes = slice(b * BLK, (b + 1) * BLK)
        ext_ref[b + 1, geo : geo + 3, :] = xyz_ref[:, lanes]
        ext_ref[b + 1, geo + 3 : geo + GEO, :] = jnp.zeros((GEO - 3, BLK), jnp.float32)
    for b in range(blocks):
        loads[b].wait()
        own = ext_ref[b + 1, TAPS:geo, :]
        parts[b] = jnp.sum((weight * own).reshape(steps // 8, 8, BLK), axis=0)
    turned[1] = turn(ext_ref[1, geo : geo + GEO, :])
    fill(even, even_sample, turned[1], ext_ref[1, geo : geo + GEO, :])
    pl.semaphore_wait(barrier, len(peers))
    inner = pl.ds(TAPS, steps + GEO)
    tail = pl.ds(steps, TAPS)
    head = pl.ds(0, TAPS)
    middle = pl.ds(1, blocks)
    moves = [
        (0, 1, ext_ref.at[blocks, inner], ext_ref.at[0, inner]),
        (0, -1, ext_ref.at[1, inner], ext_ref.at[blocks + 1, inner]),
        (1, 0, ext_ref.at[middle, tail], ext_ref.at[middle, head]),
        (1, 1, ext_ref.at[blocks, tail], ext_ref.at[0, head]),
        (1, -1, ext_ref.at[1, tail], ext_ref.at[blocks + 1, head]),
    ]
    for s, d in peers:
        if d == 0:
            moves.append((s, d, parts, slots.at[s, middle]))
        elif d == 1:
            moves.append((s, d, parts.at[blocks - 1], slots.at[s, 0]))
        else:
            moves.append((s, d, parts.at[0], slots.at[s, blocks + 1]))
    copies = []
    for i, (s, d, source, target) in enumerate(moves):
        copy = pltpu.make_async_remote_copy(
            src_ref=source,
            dst_ref=target,
            send_sem=send.at[i],
            recv_sem=recv.at[i],
            device_id=device(s, d),
            device_id_type=pl.DeviceIdType.MESH,
        )
        copies.append(copy)
    for copy in copies[2:] + copies[:2]:
        copy.start()
    for c in range(1, blocks + 1):
        shift(high, low, ext_ref, c, TAPS, steps + HALF - TAPS)
    acc[...] = jnp.zeros_like(acc)
    last[...] = jnp.zeros_like(last)
    local = lax.broadcasted_iota(jnp.int32, (steps, BLK), 0)
    growth = jnp.exp((position * steps + local).astype(jnp.float32) * -math.log(damping)) / NT
    growth = jnp.where(local % 2 == 0, -growth, growth)
    for copy, c in zip(copies[:2], (0, blocks + 1)):
        copy.wait()
        shift(high, low, ext_ref, c, TAPS, steps + HALF - TAPS)
    for copy in copies[2:]:
        copy.wait()
    around = jnp.where(position == 0, math.exp(NT * math.log(damping)), 1.0)
    for c in range(blocks + 2):
        ext_ref[c, :TAPS, :] = ext_ref[c, :TAPS, :] * around
        total = parts[c - 1] if 1 <= c <= blocks else slots[0, c]
        for s in range(1, groups):
            total = total + slots[s, c]
        place = lax.broadcasted_iota(jnp.int32, (GEO, BLK), 0)
        total = jnp.sum(total, axis=0, keepdims=True)
        turned[c] = turn(jnp.where(place == 3, total, ext_ref[c, geo : geo + GEO, :]))
        shift(high, low, ext_ref, c, 0, TAPS)
    pairs = list_ref.shape[1]

    def step(slot, now, now_sample, later, later_sample):
        following = jnp.minimum(slot + 1, pairs - 1)
        row = list_ref[0, following]
        col = list_ref[1, following]
        mine = ext_ref[row + 1, geo : geo + GEO, :]
        theirs = turned[col]
        col = list_ref[1, slot]
        total = contract(high, low, now, col, steps)
        sums = jnp.sum(now_sample[...] * turned[col][:, 3:4], axis=0, keepdims=True)
        fill(later, later_sample, theirs, mine)
        target = jnp.where(slot < count_ref[0], list_ref[0, slot], blocks)
        for r in range(blocks):
            acc[r] = acc[r] + jnp.where(target == r, total, 0.0)
            last[r] = last[r] + jnp.where(target == r, sums, 0.0)

    def two(i, carry):
        step(2 * i, even, even_sample, odd, odd_sample)
        step(2 * i + 1, odd, odd_sample, even, even_sample)
        return carry

    lax.fori_loop(0, pairs // 2, two, 0)
    for r in range(blocks):
        out_ref[:, r * BLK : (r + 1) * BLK] = acc[r] + growth * last[r, 0:1, :]


def per_device(traces, centroids, near_list, pair_count):
    steps, width = traces.shape
    blocks = width // BLK
    groups = lax.axis_size("freq")
    count = 5 + 3 * groups - 1
    depth = (HALF + 2 * PAIR) * BLK
    vmem = pl.BlockSpec(memory_space=pltpu.VMEM)
    smem = pl.BlockSpec(memory_space=pltpu.SMEM)
    return pl.pallas_call(
        operator,
        out_shape=jax.ShapeDtypeStruct((steps, width), jnp.float32),
        in_specs=[smem, smem, pl.BlockSpec(memory_space=pltpu.HBM), vmem],
        out_specs=vmem,
        scratch_shapes=[
            pltpu.VMEM((blocks + 2, TAPS + steps + GEO, BLK), jnp.float32),
            pltpu.VMEM((blocks + 2, steps + HALF, HALF * BLK), jnp.bfloat16),
            pltpu.VMEM((blocks + 2, steps + HALF, PAIR * BLK), jnp.bfloat16),
            pltpu.VMEM((depth, 2 * BLK), jnp.bfloat16),
            pltpu.VMEM((depth, 2 * BLK), jnp.bfloat16),
            pltpu.VMEM((BLK, BLK), jnp.float32),
            pltpu.VMEM((BLK, BLK), jnp.float32),
            pltpu.VMEM((blocks + 2, BLK, BLK), jnp.float32),
            pltpu.VMEM((blocks, steps, BLK), jnp.float32),
            pltpu.VMEM((blocks, 8, BLK), jnp.float32),
            pltpu.VMEM((blocks, 8, BLK), jnp.float32),
            pltpu.VMEM((groups, blocks + 2, 8, BLK), jnp.float32),
            pltpu.SemaphoreType.DMA((count,)),
            pltpu.SemaphoreType.DMA((count,)),
            pltpu.SemaphoreType.DMA((blocks,)),
        ],
        compiler_params=pltpu.CompilerParams(
            collective_id=0, has_side_effects=True, vmem_limit_bytes=60 * 1024 * 1024
        ),
    )(near_list[0].T, pair_count, traces, centroids)


def solution(mesh):
    in_specs = (
        P("freq", ("grp", "panel")),
        P(None, ("grp", "panel")),
        P(("grp", "panel"), None, None),
        P(("grp", "panel")),
    )
    out_specs = P("freq", ("grp", "panel"))
    return jax.shard_map(
        per_device, mesh=mesh, in_specs=in_specs, out_specs=out_specs, check_vma=False
    )
```
